32 devices in a mesh: gx: 2 (over core), gy: 4 (over y, x), gz: 4 (over z).
Axes of the slice: x: 2, y: 2, z: 4, core: 2. Of those that a mesh axis runs over, the one named last changes fastest.
Arguments:
- right_side: float32 [64, 512, 256], P('gx', 'gy', 'gz'), may hold values from -21 to 21, as said below
- conductivity: float32 [64, 512, 256], P('gx', 'gy', 'gz'), may hold values from 0.25 to 1
- absorption: float32 [64, 512, 256], P('gx', 'gy', 'gz'), may hold values from 0.5 to 2
Outputs:
- solution_field: float32 [64, 512, 256], P('gx', 'gy', 'gz')
- residual: float32 [64, 512, 256], P('gx', 'gy', 'gz')
The draws below stay inside these ranges and needn't reach their ends.
Inputs may be any that keep to these rules, and one draw needn't show every extreme that they name: right_side lies within -21 and 21.
All inputs are finite; a program needn't handle non-finite values.
Results may differ from the reference program's by a relative error of at most 0.004.
Values sent between devices are 32-bit elements.
A program may use at most 128 MiB of HBM per device.

```python
import math
import jax
import jax.numpy as jnp

ITERS = 10
NX = 64
NY = 512
NZ = 256


def draw_right_side(key, part):
    noise_key = jax.random.fold_in(key, 11)
    phase_key = jax.random.fold_in(key, 23)
    noise = jnp.clip(jax.random.normal(noise_key, (NX, NY, NZ), jnp.float32), -6.0, 6.0)
    phases = jax.random.uniform(phase_key, (3,), jnp.float32, 0.0, 2.0 * math.pi)
    along_x = jnp.arange(NX, dtype=jnp.float32) / NX
    along_y = jnp.arange(NY, dtype=jnp.float32) / NY
    along_z = jnp.arange(NZ, dtype=jnp.float32) / NZ
    wave_x = 0.5 + 0.5 * jnp.cos(2.0 * math.pi * along_x + phases[0])
    wave_y = 0.5 + 0.5 * jnp.cos(2.0 * math.pi * along_y + phases[1])
    wave_z = 0.5 + 0.5 * jnp.cos(2.0 * math.pi * along_z + phases[2])
    envelope = 0.4 + 3.0 * wave_x[:, None, None] * wave_y[None, :, None] * wave_z[None, None, :]
    return noise * envelope


def block_levels(rng, extent, pieces, low, largest):
    level = 1.0
    for position, blocks in pieces:
        steps = jax.random.uniform(jax.random.fold_in(jax.random.fold_in(rng, 6), position), (blocks,), jnp.float32, low / len(pieces), largest / len(pieces))
        level = level * jnp.repeat(jnp.exp(steps), extent[position] // blocks).reshape((-1,) + (1,) * (len(extent) - 1 - position))
    return level


def setup_inputs(seed: int = 0) -> dict:
    seeds = jax.random.split(jax.random.key(seed), 4)
    return {
        "right_side": draw_right_side(jax.random.fold_in(seeds[3], 71), 0),
        "conductivity": jnp.clip(jnp.exp(math.log(1.0) - 1.3862944 * jax.random.uniform(seeds[1], (NX, NY, NZ), jnp.float32) ** block_levels(seeds[1], (NX, NY, NZ), ((0, 2), (1, 4), (2, 4)), -0.2, 0.2)), 0.25, 1.0),
        "absorption": jnp.clip(0.5 + 1.5 * jax.random.uniform(seeds[2], (NX, NY, NZ), jnp.float32) ** block_levels(seeds[2], (NX, NY, NZ), ((0, 2), (1, 4), (2, 4)), -0.2, 0.2), 0.5, 2.0),
    }


def coefficients(conductivity, absorption):
    padded = jnp.pad(conductivity, 1)
    face_x = 0.5 * (padded[:-1, 1:-1, 1:-1] + padded[1:, 1:-1, 1:-1])
    face_y = 0.5 * (padded[1:-1, :-1, 1:-1] + padded[1:-1, 1:, 1:-1])
    face_z = 0.5 * (padded[1:-1, 1:-1, :-1] + padded[1:-1, 1:-1, 1:])
    total = absorption + face_x[1:] + face_x[:-1] + face_y[:, 1:] + face_y[:, :-1] + face_z[:, :, 1:] + face_z[:, :, :-1]
    return face_x, face_y, face_z, total


def operate(field, coeffs):
    face_x, face_y, face_z, total = coeffs
    padded = jnp.pad(field, 1)
    beside = face_x[1:] * padded[2:, 1:-1, 1:-1] + face_x[:-1] * padded[:-2, 1:-1, 1:-1]
    beside = beside + face_y[:, 1:] * padded[1:-1, 2:, 1:-1] + face_y[:, :-1] * padded[1:-1, :-2, 1:-1]
    beside = beside + face_z[:, :, 1:] * padded[1:-1, 1:-1, 2:] + face_z[:, :, :-1] * padded[1:-1, 1:-1, :-2]
    return total * field - beside


def reference(right_side, conductivity, absorption):
    coeffs = coefficients(conductivity, absorption)
    total = coeffs[3]
    solution_field = jnp.zeros_like(right_side)
    residual = right_side
    precond = residual / total
    direction = precond
    rho_now = jnp.sum(residual * precond)
    for iteration in range(ITERS):
        image = operate(direction, coeffs)
        step_size = rho_now / jnp.sum(direction * image)
        solution_field = solution_field + step_size * direction
        residual = residual - step_size * image
        precond = residual / total
        rho_next = jnp.sum(residual * precond)
        direction = precond + (rho_next / rho_now) * direction
        rho_now = rho_next
    return solution_field, residual
```

```python
import functools

import jax
import jax.numpy as jnp
from jax import lax
from jax.experimental import pallas as pl
from jax.experimental.pallas import tpu as pltpu
from jax.sharding import PartitionSpec as P

ITERS = 10
SIGMA = 0.75
AXES = ("gx", "gy", "gz")
MESH = pl.DeviceIdType.MESH
PAD = 8
TILE = 8
LANES = 128
HALF = LANES // 2
MOMENT_ROWS = 24


def krylov_coefficients(moments):
    zero = jnp.zeros_like(moments[0])
    one = zero + 1.0

    def shifted(values):
        out = [SIGMA * values[1]]
        for j in range(1, len(values) - 1):
            out.append(0.5 * SIGMA * (values[j + 1] + values[j - 1]))
        return out

    def times_j(coeffs):
        out = [zero] * (len(coeffs) + 1)
        for j, value in enumerate(coeffs):
            if j == 0:
                out[1] = out[1] + SIGMA * value
            else:
                out[j + 1] = out[j + 1] + 0.5 * SIGMA * value
                out[j - 1] = out[j - 1] + 0.5 * SIGMA * value
        return out

    z_dots, p_dots = list(moments), list(moments)
    z_poly, p_poly, x_poly = [one], [one], []
    rho = moments[0]
    for k in range(ITERS):
        moved = shifted(p_dots)
        image_dots = [p_dots[j] - moved[j] for j in range(len(moved))]
        moved = times_j(p_poly)
        image_poly = [(p_poly[j] if j <= k else zero) - moved[j] for j in range(k + 2)]
        product = p_poly[k] * image_dots[k]
        good = jnp.logical_and(rho > 0.0, product > 0.0)
        step = jnp.where(good, rho / jnp.where(good, product, 1.0), 0.0)
        x_poly = [(x_poly[j] if j < k else zero) + step * p_poly[j] for j in range(k + 1)]
        z_poly = [(z_poly[j] if j <= k else zero) - step * image_poly[j] for j in range(k + 2)]
        z_dots = [z_dots[j] - step * image_dots[j] for j in range(len(image_dots))]
        rho_next = jnp.maximum(z_poly[k + 1] * z_dots[k + 1], 0.0)
        mixing = jnp.where(good, rho_next / jnp.where(good, rho, 1.0), 0.0)
        p_poly = [z_poly[j] + (mixing * p_poly[j] if j <= k else zero) for j in range(k + 2)]
        p_dots = [z_dots[j] + mixing * p_dots[j] for j in range(len(image_dots))]
        rho = rho_next
    return x_poly, z_poly


def kernel(sizes, b_ref, c_ref, a_ref, x_ref, r_ref,
           field, weight, diag, ysend, yrecv, yhalo, zsend, zrecv, dots,
           parts_x, parts_y, parts_z, send_sem, recv_sem, sum_send, sum_recv):
    nx, nz, ny = x_ref.shape
    tiles = nz // TILE
    per_group = HALF // tiles
    groups = nx // per_group
    me = {axis: lax.axis_index(axis) for axis in AXES}
    inner = pl.ds(PAD, nz)

    barrier = pltpu.get_barrier_semaphore()
    greeted = 0
    for axis in AXES:
        for hop in range(1, sizes[axis]):
            peer = lax.rem(me[axis] + hop, sizes[axis])
            pl.semaphore_signal(barrier, inc=1, device_id={axis: peer}, device_id_type=MESH)
            greeted += 1
    pl.semaphore_wait(barrier, greeted)

    lane = lax.broadcasted_iota(jnp.int32, (TILE, LANES), 1)
    owner = ((lane + 1) // 2) % HALF
    even = lane % 2 == 0
    lane_wide = lax.broadcasted_iota(jnp.int32, (nz, LANES), 1)
    first, last = lane_wide == 0, lane_wide == LANES - 1

    def each_copy(slot, act):
        plan = {
            "gx": ((field.at[slot, 1, inner], field.at[slot, nx + 1, inner]),
                   (field.at[slot, nx, inner], field.at[slot, 0, inner])),
            "gy": ((ysend.at[slot], yrecv.at[slot, 1]), (ysend.at[slot], yrecv.at[slot, 0])),
            "gz": ((zsend.at[slot, 0], zrecv.at[slot, 1]), (zsend.at[slot, 1], zrecv.at[slot, 0])),
        }
        for number, axis in enumerate(AXES):
            for side in range(2):
                source, target = plan[axis][side]
                act(axis, side, source, target, slot, 2 * number + side)

    def descriptor(axis, side, source, target, slot, index):
        peer = me[axis] + (2 * side - 1)
        return pltpu.make_async_remote_copy(
            src_ref=source, dst_ref=target,
            send_sem=send_sem.at[slot, index], recv_sem=recv_sem.at[slot, index],
            device_id={axis: peer}, device_id_type=MESH)

    def has_peer(axis, side):
        return me[axis] > 0 if side == 0 else me[axis] < sizes[axis] - 1

    def start(axis, side, *rest):
        @pl.when(has_peer(axis, side))
        def _():
            descriptor(axis, side, *rest).start()

    def finish(axis, side, *rest):
        @pl.when(has_peer(axis, side))
        def _():
            descriptor(axis, side, *rest).wait_send()

        @pl.when(has_peer(axis, 1 - side))
        def _():
            descriptor(axis, side, *rest).wait_recv()

    def clear(slot, carry):
        plane = jnp.zeros((nz, ny), jnp.float32)
        for edge, at in ((me["gx"] == 0, 0), (me["gx"] == sizes["gx"] - 1, nx + 1)):
            @pl.when(edge)
            def _():
                field[slot, at, inner] = plane
        for edge, at in ((me["gy"] == 0, 0), (me["gy"] == sizes["gy"] - 1, 1)):
            @pl.when(edge)
            def _():
                yrecv[slot, at] = jnp.zeros(yrecv.shape[2:], jnp.float32)
        for edge, at in ((me["gz"] == 0, 0), (me["gz"] == sizes["gz"] - 1, 1)):
            @pl.when(edge)
            def _():
                zrecv[slot, at] = jnp.zeros(zrecv.shape[2:], jnp.float32)
        return carry

    lax.fori_loop(0, ITERS + 1, clear, 0)

    def put(slot, x, within, plane, packed):
        field[slot, x + 1, inner] = plane
        zsend[slot, 0, pl.ds(x, 1)] = plane[:1]
        zsend[slot, 1, pl.ds(x, 1)] = plane[nz - 1:]
        for tile in range(tiles):
            number = within * tiles + tile
            part = plane[tile * TILE:(tile + 1) * TILE]
            if number:
                part = pltpu.roll(part, 2 * number, 1)
            packed = jnp.where(owner == number, part, packed)
        return packed

    def exchange(slot):
        each_copy(slot, start)
        each_copy(slot, finish)
        for group in range(groups):
            yhalo[group] = jnp.where(even, pltpu.roll(yrecv[slot, 0, group], 1, 1),
                                     pltpu.roll(yrecv[slot, 1, group], LANES - 1, 1))
        for x in range(nx):
            field[slot, x + 1, PAD - 1:PAD] = zrecv[slot, 0, x:x + 1]
            field[slot, x + 1, PAD + nz:PAD + nz + 1] = zrecv[slot, 1, x:x + 1]

    def around(slot, x, group, within):
        here = field[slot, x + 1, inner]
        beside = yhalo[group]
        edge = []
        for tile in range(tiles):
            number = within * tiles + tile
            edge.append(pltpu.roll(beside, LANES - 2 * number, 1) if number else beside)
        edge = jnp.concatenate(edge, axis=0)
        return here, (
            field[slot, x + 2, inner],
            field[slot, x, inner],
            jnp.where(last, edge, pltpu.roll(here, LANES - 1, 1)),
            jnp.where(first, edge, pltpu.roll(here, 1, 1)),
            field[slot, x + 1, PAD + 1:PAD + 1 + nz],
            field[slot, x + 1, PAD - 1:PAD - 1 + nz],
        )

    def fold(plane):
        total = plane[:TILE]
        for tile in range(1, tiles):
            total = total + plane[tile * TILE:(tile + 1) * TILE]
        return total

    nothing = jnp.zeros((TILE, LANES), jnp.float32)

    def load(group, carry):
        packed = nothing
        for within in range(per_group):
            x = group * per_group + within
            packed = put(0, x, within, c_ref[x], packed)
        ysend[0, group] = packed
        return carry

    lax.fori_loop(0, groups, load, 0)
    exchange(0)

    def prepare(group, total):
        packed = nothing
        for within in range(per_group):
            x = group * per_group + within
            here, neighbours = around(0, x, group, within)
            faces = [0.5 * (here + other) for other in neighbours]
            diagonal = a_ref[x]
            for face in faces:
                diagonal = diagonal + face
            inverse = 1.0 / diagonal
            scale = (2.0 / SIGMA) * inverse
            for number, face in enumerate(faces):
                weight[number, x] = face * scale
            diag[x] = diagonal
            source = b_ref[x]
            precond = source / diagonal
            packed = put(1, x, within, precond, packed)
            total = total + fold(source * precond)
        ysend[1, group] = packed
        return total

    dots[0, 0] = lax.fori_loop(0, groups, prepare, nothing)

    def step(k, carry):
        slot = k + 1
        exchange(slot)
        scale = jnp.where(k == 0, 0.5, 1.0).astype(jnp.float32)
        keep = jnp.where(k == 0, 0.0, 1.0).astype(jnp.float32)

        def apply(group, totals):
            even_total, odd_total = totals
            packed = nothing
            for within in range(per_group):
                x = group * per_group + within
                here, neighbours = around(slot, x, group, within)
                image = weight[0, x] * neighbours[0]
                for number in range(1, 6):
                    image = image + weight[number, x] * neighbours[number]
                new = scale * image - keep * field[slot - 1, x + 1, inner]
                packed = put(slot + 1, x, within, new, packed)
                weighed = diag[x] * new
                even_total = even_total + fold(weighed * new)
                odd_total = odd_total + fold(weighed * here)
            ysend[slot + 1, group] = packed
            return even_total, odd_total

        even_total, odd_total = lax.fori_loop(0, groups, apply, (nothing, nothing))
        dots[k + 1, 0] = even_total
        dots[k, 1] = odd_total
        return carry

    lax.fori_loop(0, ITERS, step, 0)

    rows = [jnp.sum(dots[k, 0], axis=0, keepdims=True) for k in range(ITERS + 1)]
    rows += [jnp.sum(dots[k, 1], axis=0, keepdims=True) for k in range(ITERS)]
    rows += [jnp.zeros((1, LANES), jnp.float32)] * (MOMENT_ROWS - len(rows))
    sums = jnp.concatenate(rows, axis=0)
    base = 0
    for axis, parts in zip(AXES, (parts_x, parts_y, parts_z)):
        count = sizes[axis]
        parts[me[axis]] = sums
        copies = []
        for hop in range(1, count):
            copies.append(pltpu.make_async_remote_copy(
                src_ref=parts.at[me[axis]], dst_ref=parts.at[me[axis]],
                send_sem=sum_send.at[base], recv_sem=sum_recv.at[base],
                device_id={axis: lax.rem(me[axis] + hop, count)}, device_id_type=MESH))
            base += 1
        for copy in copies:
            copy.start()
        for hop, copy in enumerate(copies):
            came = lax.rem(me[axis] + (count - 1 - hop), count)
            copy.wait_send()
            pltpu.make_async_remote_copy(
                src_ref=parts.at[came], dst_ref=parts.at[came],
                send_sem=sum_send.at[base - count + 1 + hop],
                recv_sem=sum_recv.at[base - count + 1 + hop],
                device_id={axis: came}, device_id_type=MESH).wait_recv()
        sums = parts[0]
        for number in range(1, count):
            sums = sums + parts[number]

    sums = jnp.broadcast_to(jnp.sum(sums, axis=1, keepdims=True), (MOMENT_ROWS, LANES))
    evens = [sums[k:k + 1] for k in range(ITERS + 1)]
    odds = [sums[ITERS + 1 + k:ITERS + 2 + k] for k in range(ITERS)]
    moments = [evens[0], odds[0]]
    for k in range(1, ITERS + 1):
        moments.append(2.0 * evens[k] - moments[0])
        if k < ITERS:
            moments.append(2.0 * odds[k] - moments[1])
    x_poly, z_poly = krylov_coefficients(moments)

    def combine(x, carry):
        value = field[1, x + 1, inner]
        solution_field = x_poly[0] * value
        remainder = z_poly[0] * value
        for k in range(1, ITERS + 1):
            value = field[k + 1, x + 1, inner]
            if k < ITERS:
                solution_field = solution_field + x_poly[k] * value
            remainder = remainder + z_poly[k] * value
        x_ref[x] = solution_field
        r_ref[x] = remainder * diag[x]
        return carry

    lax.fori_loop(0, nx, combine, 0)


def local(sizes, right_side, conductivity, absorption):
    turned = [jnp.swapaxes(value, 1, 2) for value in (right_side, conductivity, absorption)]
    nx, nz, ny = turned[0].shape
    groups = nx * (nz // TILE) // HALF
    slots = ITERS + 2
    f32 = jnp.float32
    links = sum(sizes[axis] - 1 for axis in AXES)
    out = jax.ShapeDtypeStruct((nx, nz, ny), f32)
    vmem = pl.BlockSpec(memory_space=pltpu.VMEM)
    outs = pl.pallas_call(
        functools.partial(kernel, sizes),
        out_shape=(out, out),
        in_specs=[vmem] * 3,
        out_specs=(vmem, vmem),
        scratch_shapes=[
            pltpu.VMEM((slots, nx + 2, nz + 2 * PAD, ny), f32),
            pltpu.VMEM((6, nx, nz, ny), f32),
            pltpu.VMEM((nx, nz, ny), f32),
            pltpu.VMEM((slots, groups, TILE, LANES), f32),
            pltpu.VMEM((slots, 2, groups, TILE, LANES), f32),
            pltpu.VMEM((groups, TILE, LANES), f32),
            pltpu.VMEM((slots, 2, nx, ny), f32),
            pltpu.VMEM((slots, 2, nx, ny), f32),
            pltpu.VMEM((ITERS + 1, 2, TILE, LANES), f32),
            pltpu.VMEM((sizes["gx"], MOMENT_ROWS, LANES), f32),
            pltpu.VMEM((sizes["gy"], MOMENT_ROWS, LANES), f32),
            pltpu.VMEM((sizes["gz"], MOMENT_ROWS, LANES), f32),
            pltpu.SemaphoreType.DMA((slots, 6)),
            pltpu.SemaphoreType.DMA((slots, 6)),
            pltpu.SemaphoreType.DMA((links,)),
            pltpu.SemaphoreType.DMA((links,)),
        ],
        compiler_params=pltpu.CompilerParams(
            collective_id=0, has_side_effects=True, vmem_limit_bytes=60 * 1024 * 1024),
    )(*turned)
    return tuple(jnp.swapaxes(value, 1, 2) for value in outs)


def solution(mesh):
    sizes = dict(mesh.shape)
    return jax.shard_map(
        functools.partial(local, sizes),
        mesh=mesh,
        in_specs=(P(*AXES), P(*AXES), P(*AXES)),
        out_specs=(P(*AXES), P(*AXES)),
        check_vma=False,
    )
```

```python
import functools

import jax
import jax.numpy as jnp
from jax import lax
from jax.experimental import pallas as pl
from jax.experimental.pallas import tpu as pltpu
from jax.sharding import PartitionSpec as P

ITERS = 10
AXES = ("gx", "gy", "gz")
MESH = pl.DeviceIdType.MESH
PAD = 8
TILE = 8
LANES = 128
HALF = LANES // 2
DOT_ROWS = 8


def kernel(sizes, b_ref, c_ref, a_ref, x_ref, r_ref,
           field, weight, diag, inverse, image_ref, direction_ref, along_ref,
           ysend, yrecv, yhalo, zsend, zrecv,
           parts_x, parts_y, parts_z, send_sem, recv_sem, sum_send, sum_recv):
    nx, nz, ny = x_ref.shape
    tiles = nz // TILE
    per_group = HALF // tiles
    groups = nx // per_group
    me = {axis: lax.axis_index(axis) for axis in AXES}
    inner = pl.ds(PAD, nz)

    barrier = pltpu.get_barrier_semaphore()
    greeted = 0
    for axis in AXES:
        for hop in range(1, sizes[axis]):
            peer = lax.rem(me[axis] + hop, sizes[axis])
            pl.semaphore_signal(barrier, inc=1, device_id={axis: peer}, device_id_type=MESH)
            greeted += 1
    pl.semaphore_wait(barrier, greeted)

    lane = lax.broadcasted_iota(jnp.int32, (TILE, LANES), 1)
    owner = ((lane + 1) // 2) % HALF
    even = lane % 2 == 0
    lane_wide = lax.broadcasted_iota(jnp.int32, (nz, LANES), 1)
    first, last = lane_wide == 0, lane_wide == LANES - 1

    def each_copy(slot, act):
        plan = {
            "gx": ((field.at[slot, 1, inner], field.at[slot, nx + 1, inner]),
                   (field.at[slot, nx, inner], field.at[slot, 0, inner])),
            "gy": ((ysend.at[slot], yrecv.at[slot, 1]), (ysend.at[slot], yrecv.at[slot, 0])),
            "gz": ((zsend.at[slot, 0], zrecv.at[slot, 1]), (zsend.at[slot, 1], zrecv.at[slot, 0])),
        }
        for number, axis in enumerate(AXES):
            for side in range(2):
                source, target = plan[axis][side]
                act(axis, side, source, target, slot, 2 * number + side)

    def descriptor(axis, side, source, target, slot, index):
        peer = me[axis] + (2 * side - 1)
        return pltpu.make_async_remote_copy(
            src_ref=source, dst_ref=target,
            send_sem=send_sem.at[slot, index], recv_sem=recv_sem.at[slot, index],
            device_id={axis: peer}, device_id_type=MESH)

    def has_peer(axis, side):
        return me[axis] > 0 if side == 0 else me[axis] < sizes[axis] - 1

    def start(axis, side, *rest):
        @pl.when(has_peer(axis, side))
        def _():
            descriptor(axis, side, *rest).start()

    def finish(axis, side, *rest):
        @pl.when(has_peer(axis, side))
        def _():
            descriptor(axis, side, *rest).wait_send()

        @pl.when(has_peer(axis, 1 - side))
        def _():
            descriptor(axis, side, *rest).wait_recv()

    def clear(slot, carry):
        plane = jnp.zeros((nz, ny), jnp.float32)
        for edge, at in ((me["gx"] == 0, 0), (me["gx"] == sizes["gx"] - 1, nx + 1)):
            @pl.when(edge)
            def _():
                field[slot, at, inner] = plane
        for edge, at in ((me["gy"] == 0, 0), (me["gy"] == sizes["gy"] - 1, 1)):
            @pl.when(edge)
            def _():
                yrecv[slot, at] = jnp.zeros(yrecv.shape[2:], jnp.float32)
        for edge, at in ((me["gz"] == 0, 0), (me["gz"] == sizes["gz"] - 1, 1)):
            @pl.when(edge)
            def _():
                zrecv[slot, at] = jnp.zeros(zrecv.shape[2:], jnp.float32)
        return carry

    lax.fori_loop(0, ITERS + 1, clear, 0)

    def put(slot, x, within, plane, packed):
        field[slot, x + 1, inner] = plane
        zsend[slot, 0, pl.ds(x, 1)] = plane[:1]
        zsend[slot, 1, pl.ds(x, 1)] = plane[nz - 1:]
        for tile in range(tiles):
            number = within * tiles + tile
            part = plane[tile * TILE:(tile + 1) * TILE]
            if number:
                part = pltpu.roll(part, 2 * number, 1)
            packed = jnp.where(owner == number, part, packed)
        return packed

    def exchange(slot):
        each_copy(slot, start)
        each_copy(slot, finish)
        for group in range(groups):
            yhalo[group] = jnp.where(even, pltpu.roll(yrecv[slot, 0, group], 1, 1),
                                     pltpu.roll(yrecv[slot, 1, group], LANES - 1, 1))
        for x in range(nx):
            field[slot, x + 1, PAD - 1:PAD] = zrecv[slot, 0, x:x + 1]
            field[slot, x + 1, PAD + nz:PAD + nz + 1] = zrecv[slot, 1, x:x + 1]

    def around(slot, x, group, within):
        here = field[slot, x + 1, inner]
        beside = yhalo[group]
        edge = []
        for tile in range(tiles):
            number = within * tiles + tile
            edge.append(pltpu.roll(beside, LANES - 2 * number, 1) if number else beside)
        edge = jnp.concatenate(edge, axis=0)
        return here, (
            field[slot, x + 2, inner],
            field[slot, x, inner],
            jnp.where(last, edge, pltpu.roll(here, LANES - 1, 1)),
            jnp.where(first, edge, pltpu.roll(here, 1, 1)),
            field[slot, x + 1, PAD + 1:PAD + 1 + nz],
            field[slot, x + 1, PAD - 1:PAD - 1 + nz],
        )

    def fold(plane):
        total = plane[:TILE]
        for tile in range(1, tiles):
            total = total + plane[tile * TILE:(tile + 1) * TILE]
        return total

    nothing = jnp.zeros((TILE, LANES), jnp.float32)

    def load(group, carry):
        packed = nothing
        for within in range(per_group):
            x = group * per_group + within
            packed = put(0, x, within, c_ref[x], packed)
        ysend[0, group] = packed
        return carry

    lax.fori_loop(0, groups, load, 0)
    exchange(0)

    def prepare(group, carry):
        packed = nothing
        for within in range(per_group):
            x = group * per_group + within
            here, neighbours = around(0, x, group, within)
            faces = [0.5 * (here + other) for other in neighbours]
            diagonal = a_ref[x]
            for number, face in enumerate(faces):
                diagonal = diagonal + face
                weight[number, x] = face
            diag[x] = diagonal
            reciprocal = 1.0 / diagonal
            inverse[x] = reciprocal
            source = b_ref[x]
            r_ref[x] = source
            blank = jnp.zeros_like(source)
            x_ref[x] = blank
            direction_ref[x] = blank
            along_ref[x] = blank
            packed = put(1, x, within, source * reciprocal, packed)
        ysend[1, group] = packed
        return carry

    lax.fori_loop(0, groups, prepare, 0)

    def all_sums(k, sums):
        base = 0
        for axis, parts in zip(AXES, (parts_x, parts_y, parts_z)):
            count = sizes[axis]
            parts[k, me[axis]] = sums
            sends, arrivals = [], []
            for hop in range(1, count):
                for whose, device, out in (
                    (me[axis], lax.rem(me[axis] + hop, count), sends),
                    (lax.rem(me[axis] + count - hop, count),) * 2 + (arrivals,),
                ):
                    out.append(pltpu.make_async_remote_copy(
                        src_ref=parts.at[k, whose], dst_ref=parts.at[k, whose],
                        send_sem=sum_send.at[k, base], recv_sem=sum_recv.at[k, base],
                        device_id={axis: device}, device_id_type=MESH))
                base += 1
            for copy in sends:
                copy.start()
            for copy, arrival in zip(sends, arrivals):
                copy.wait_send()
                arrival.wait_recv()
            sums = parts[k, 0]
            for number in range(1, count):
                sums = sums + parts[k, number]
        return jnp.broadcast_to(jnp.sum(sums, axis=1, keepdims=True), (DOT_ROWS, LANES))

    def iteration(k, carry):
        rho_now, step_size = carry
        slot = k + 1
        exchange(slot)

        def apply(group, totals):
            rho_total, product_total = totals
            for within in range(per_group):
                x = group * per_group + within
                here, neighbours = around(slot, x, group, within)
                beside = weight[0, x] * neighbours[0]
                for number in range(1, 6):
                    beside = beside + weight[number, x] * neighbours[number]
                image = diag[x] * here - beside
                image_ref[x] = image
                rho_total = rho_total + fold(r_ref[x] * here)
                product_total = product_total + fold(image * here)
            return rho_total, product_total

        rho_total, product_total = lax.fori_loop(0, groups, apply, (nothing, nothing))
        sums = all_sums(k, jnp.concatenate([
            jnp.sum(rho_total, axis=0, keepdims=True),
            jnp.sum(product_total, axis=0, keepdims=True),
            jnp.zeros((DOT_ROWS - 2, LANES), jnp.float32)], axis=0))
        rho_next, product = sums[:1], sums[1:2]
        mixing = jnp.where(k == 0, 0.0, rho_next / rho_now)
        step_next = rho_next / (product - mixing * rho_next / step_size)

        def update(group, carry):
            packed = nothing
            for within in range(per_group):
                x = group * per_group + within
                direction = field[slot, x + 1, inner] + mixing * direction_ref[x]
                along = image_ref[x] + mixing * along_ref[x]
                direction_ref[x] = direction
                along_ref[x] = along
                x_ref[x] = x_ref[x] + step_next * direction
                residual = r_ref[x] - step_next * along
                r_ref[x] = residual
                packed = put(slot + 1, x, within, residual * inverse[x], packed)
            ysend[slot + 1, group] = packed
            return carry

        lax.fori_loop(0, groups, update, 0)
        return rho_next, step_next

    one = jnp.ones((1, LANES), jnp.float32)
    lax.fori_loop(0, ITERS, iteration, (one, one))


def local(sizes, right_side, conductivity, absorption):
    turned = [jnp.swapaxes(value, 1, 2) for value in (right_side, conductivity, absorption)]
    nx, nz, ny = turned[0].shape
    groups = nx * (nz // TILE) // HALF
    slots = ITERS + 2
    f32 = jnp.float32
    links = sum(sizes[axis] - 1 for axis in AXES)
    out = jax.ShapeDtypeStruct((nx, nz, ny), f32)
    vmem = pl.BlockSpec(memory_space=pltpu.VMEM)
    outs = pl.pallas_call(
        functools.partial(kernel, sizes),
        out_shape=(out, out),
        in_specs=[vmem] * 3,
        out_specs=(vmem, vmem),
        scratch_shapes=[
            pltpu.VMEM((slots, nx + 2, nz + 2 * PAD, ny), f32),
            pltpu.VMEM((6, nx, nz, ny), f32),
            *[pltpu.VMEM((nx, nz, ny), f32) for _ in range(5)],
            pltpu.VMEM((slots, groups, TILE, LANES), f32),
            pltpu.VMEM((slots, 2, groups, TILE, LANES), f32),
            pltpu.VMEM((groups, TILE, LANES), f32),
            pltpu.VMEM((slots, 2, nx, ny), f32),
            pltpu.VMEM((slots, 2, nx, ny), f32),
            pltpu.VMEM((ITERS, sizes["gx"], DOT_ROWS, LANES), f32),
            pltpu.VMEM((ITERS, sizes["gy"], DOT_ROWS, LANES), f32),
            pltpu.VMEM((ITERS, sizes["gz"], DOT_ROWS, LANES), f32),
            pltpu.SemaphoreType.DMA((slots, 6)),
            pltpu.SemaphoreType.DMA((slots, 6)),
            pltpu.SemaphoreType.DMA((ITERS, links)),
            pltpu.SemaphoreType.DMA((ITERS, links)),
        ],
        compiler_params=pltpu.CompilerParams(
            collective_id=0, has_side_effects=True, vmem_limit_bytes=60 * 1024 * 1024),
    )(*turned)
    return tuple(jnp.swapaxes(value, 1, 2) for value in outs)


def solution(mesh):
    sizes = dict(mesh.shape)
    return jax.shard_map(
        functools.partial(local, sizes),
        mesh=mesh,
        in_specs=(P(*AXES), P(*AXES), P(*AXES)),
        out_specs=(P(*AXES), P(*AXES)),
        check_vma=False,
    )
```

```python
import functools
import math

import jax
import jax.numpy as jnp
from jax import lax
from jax.experimental import pallas as pl
from jax.experimental.pallas import tpu as pltpu
from jax.sharding import PartitionSpec as P

ITERS = 10
AXES = ("gx", "gy", "gz")
STAGES = (("gx", "gy"), ("gz",))
MESH = pl.DeviceIdType.MESH
PAD = 8
TILE = 8
LANES = 128
HALF = LANES // 2
DOT_ROWS = 8


def kernel(sizes, b_ref, c_ref, a_ref, x_ref, r_ref,
           field, weight, diag, inverse, image_ref, direction_ref, along_ref,
           ysend, yrecv, yhalo, zsend, zrecv,
           parts_first, parts_last, send_sem, recv_sem, sum_send, sum_recv):
    nx, nz, ny = x_ref.shape
    tiles = nz // TILE
    per_group = HALF // tiles
    groups = nx // per_group
    me = {axis: lax.axis_index(axis) for axis in AXES}
    inner = pl.ds(PAD, nz)

    barrier = pltpu.get_barrier_semaphore()
    def mine(axes):
        index, count = 0, 1
        for axis in axes:
            index = index * sizes[axis] + me[axis]
            count = count * sizes[axis]
        return index, count

    def place(axes, index):
        where = {}
        for axis in reversed(axes):
            where[axis] = lax.rem(index, sizes[axis])
            index = lax.div(index, sizes[axis])
        return where

    greeted = 0
    for axes in STAGES:
        index, count = mine(axes)
        for hop in range(1, count):
            peer = place(axes, lax.rem(index + hop, count))
            pl.semaphore_signal(barrier, inc=1, device_id=peer, device_id_type=MESH)
            greeted += 1
    pl.semaphore_wait(barrier, greeted)

    lane = lax.broadcasted_iota(jnp.int32, (TILE, LANES), 1)
    owner = ((lane + 1) // 2) % HALF
    even = lane % 2 == 0
    lane_wide = lax.broadcasted_iota(jnp.int32, (nz, LANES), 1)
    first, last = lane_wide == 0, lane_wide == LANES - 1

    def each_copy(slot, act):
        plan = {
            "gx": ((field.at[slot, 1, inner], field.at[slot, nx + 1, inner]),
                   (field.at[slot, nx, inner], field.at[slot, 0, inner])),
            "gy": ((ysend.at[slot], yrecv.at[slot, 1]), (ysend.at[slot], yrecv.at[slot, 0])),
            "gz": ((zsend.at[slot, 0], zrecv.at[slot, 1]), (zsend.at[slot, 1], zrecv.at[slot, 0])),
        }
        for number, axis in enumerate(AXES):
            for side in range(2):
                source, target = plan[axis][side]
                act(axis, side, source, target, slot, 2 * number + side)

    def descriptor(axis, side, source, target, slot, index):
        peer = me[axis] + (2 * side - 1)
        return pltpu.make_async_remote_copy(
            src_ref=source, dst_ref=target,
            send_sem=send_sem.at[slot, index], recv_sem=recv_sem.at[slot, index],
            device_id={axis: peer}, device_id_type=MESH)

    def has_peer(axis, side):
        return me[axis] > 0 if side == 0 else me[axis] < sizes[axis] - 1

    def start(axis, side, *rest):
        @pl.when(has_peer(axis, side))
        def _():
            descriptor(axis, side, *rest).start()

    def finish(axis, side, *rest):
        @pl.when(has_peer(axis, side))
        def _():
            descriptor(axis, side, *rest).wait_send()

        @pl.when(has_peer(axis, 1 - side))
        def _():
            descriptor(axis, side, *rest).wait_recv()

    def clear(slot, carry):
        plane = jnp.zeros((nz, ny), jnp.float32)
        for edge, at in ((me["gx"] == 0, 0), (me["gx"] == sizes["gx"] - 1, nx + 1)):
            @pl.when(edge)
            def _():
                field[slot, at, inner] = plane
        for edge, at in ((me["gy"] == 0, 0), (me["gy"] == sizes["gy"] - 1, 1)):
            @pl.when(edge)
            def _():
                yrecv[slot, at] = jnp.zeros(yrecv.shape[2:], jnp.float32)
        for edge, at in ((me["gz"] == 0, 0), (me["gz"] == sizes["gz"] - 1, 1)):
            @pl.when(edge)
            def _():
                zrecv[slot, at] = jnp.zeros(zrecv.shape[2:], jnp.float32)
        return carry

    lax.fori_loop(0, ITERS + 1, clear, 0)

    def put(slot, x, within, plane, packed):
        field[slot, x + 1, inner] = plane
        zsend[slot, 0, pl.ds(x, 1)] = plane[:1]
        zsend[slot, 1, pl.ds(x, 1)] = plane[nz - 1:]
        for tile in range(tiles):
            number = within * tiles + tile
            part = plane[tile * TILE:(tile + 1) * TILE]
            if number:
                part = pltpu.roll(part, 2 * number, 1)
            packed = jnp.where(owner == number, part, packed)
        return packed

    def exchange(slot):
        each_copy(slot, start)
        each_copy(slot, finish)
        for group in range(groups):
            yhalo[group] = jnp.where(even, pltpu.roll(yrecv[slot, 0, group], 1, 1),
                                     pltpu.roll(yrecv[slot, 1, group], LANES - 1, 1))
        for x in range(nx):
            field[slot, x + 1, PAD - 1:PAD] = zrecv[slot, 0, x:x + 1]
            field[slot, x + 1, PAD + nz:PAD + nz + 1] = zrecv[slot, 1, x:x + 1]

    def around(slot, x, group, within):
        here = field[slot, x + 1, inner]
        beside = yhalo[group]
        edge = []
        for tile in range(tiles):
            number = within * tiles + tile
            edge.append(pltpu.roll(beside, LANES - 2 * number, 1) if number else beside)
        edge = jnp.concatenate(edge, axis=0)
        return here, (
            field[slot, x + 2, inner],
            field[slot, x, inner],
            jnp.where(last, edge, pltpu.roll(here, LANES - 1, 1)),
            jnp.where(first, edge, pltpu.roll(here, 1, 1)),
            field[slot, x + 1, PAD + 1:PAD + 1 + nz],
            field[slot, x + 1, PAD - 1:PAD - 1 + nz],
        )

    def fold(plane):
        total = plane[:TILE]
        for tile in range(1, tiles):
            total = total + plane[tile * TILE:(tile + 1) * TILE]
        return total

    nothing = jnp.zeros((TILE, LANES), jnp.float32)

    def load(group, carry):
        packed = nothing
        for within in range(per_group):
            x = group * per_group + within
            packed = put(0, x, within, c_ref[x], packed)
        ysend[0, group] = packed
        return carry

    lax.fori_loop(0, groups, load, 0)
    exchange(0)

    def prepare(group, carry):
        packed = nothing
        for within in range(per_group):
            x = group * per_group + within
            here, neighbours = around(0, x, group, within)
            faces = [0.5 * (here + other) for other in neighbours]
            diagonal = a_ref[x]
            for number, face in enumerate(faces):
                diagonal = diagonal + face
                weight[number, x] = face
            diag[x] = diagonal
            reciprocal = 1.0 / diagonal
            inverse[x] = reciprocal
            source = b_ref[x]
            r_ref[x] = source
            blank = jnp.zeros_like(source)
            x_ref[x] = blank
            direction_ref[x] = blank
            along_ref[x] = blank
            packed = put(1, x, within, source * reciprocal, packed)
        ysend[1, group] = packed
        return carry

    lax.fori_loop(0, groups, prepare, 0)

    def all_sums(k, sums):
        base = 0
        for axes, parts in zip(STAGES, (parts_first, parts_last)):
            index, count = mine(axes)
            parts[k, index] = sums
            sends, arrivals = [], []
            for hop in range(1, count):
                behind = lax.rem(index + count - hop, count)
                ahead = lax.rem(index + hop, count)
                for whose, device, out in ((index, ahead, sends), (behind, behind, arrivals)):
                    out.append(pltpu.make_async_remote_copy(
                        src_ref=parts.at[k, whose], dst_ref=parts.at[k, whose],
                        send_sem=sum_send.at[k, base], recv_sem=sum_recv.at[k, base],
                        device_id=place(axes, device), device_id_type=MESH))
                base += 1
            for copy in sends:
                copy.start()
            for copy, arrival in zip(sends, arrivals):
                copy.wait_send()
                arrival.wait_recv()
            sums = parts[k, 0]
            for number in range(1, count):
                sums = sums + parts[k, number]
        return jnp.broadcast_to(jnp.sum(sums, axis=1, keepdims=True), (DOT_ROWS, LANES))

    def iteration(k, carry):
        rho_now, step_size = carry
        slot = k + 1
        exchange(slot)

        def apply(group, totals):
            rho_total, product_total = totals
            for within in range(per_group):
                x = group * per_group + within
                here, neighbours = around(slot, x, group, within)
                beside = weight[0, x] * neighbours[0]
                for number in range(1, 6):
                    beside = beside + weight[number, x] * neighbours[number]
                image = diag[x] * here - beside
                image_ref[x] = image
                rho_total = rho_total + fold(r_ref[x] * here)
                product_total = product_total + fold(image * here)
            return rho_total, product_total

        rho_total, product_total = lax.fori_loop(0, groups, apply, (nothing, nothing))
        sums = all_sums(k, jnp.concatenate([
            jnp.sum(rho_total, axis=0, keepdims=True),
            jnp.sum(product_total, axis=0, keepdims=True),
            jnp.zeros((DOT_ROWS - 2, LANES), jnp.float32)], axis=0))
        rho_next, product = sums[:1], sums[1:2]
        mixing = jnp.where(k == 0, 0.0, rho_next / rho_now)
        step_next = rho_next / (product - mixing * rho_next / step_size)

        def update(group, carry):
            packed = nothing
            for within in range(per_group):
                x = group * per_group + within
                direction = field[slot, x + 1, inner] + mixing * direction_ref[x]
                along = image_ref[x] + mixing * along_ref[x]
                direction_ref[x] = direction
                along_ref[x] = along
                x_ref[x] = x_ref[x] + step_next * direction
                residual = r_ref[x] - step_next * along
                r_ref[x] = residual
                packed = put(slot + 1, x, within, residual * inverse[x], packed)
            ysend[slot + 1, group] = packed
            return carry

        lax.fori_loop(0, groups, update, 0)
        return rho_next, step_next

    one = jnp.ones((1, LANES), jnp.float32)
    lax.fori_loop(0, ITERS, iteration, (one, one))


def local(sizes, right_side, conductivity, absorption):
    turned = [jnp.swapaxes(value, 1, 2) for value in (right_side, conductivity, absorption)]
    nx, nz, ny = turned[0].shape
    groups = nx * (nz // TILE) // HALF
    slots = ITERS + 2
    f32 = jnp.float32
    counts = [math.prod(sizes[axis] for axis in axes) for axes in STAGES]
    links = sum(count - 1 for count in counts)
    out = jax.ShapeDtypeStruct((nx, nz, ny), f32)
    vmem = pl.BlockSpec(memory_space=pltpu.VMEM)
    outs = pl.pallas_call(
        functools.partial(kernel, sizes),
        out_shape=(out, out),
        in_specs=[vmem] * 3,
        out_specs=(vmem, vmem),
        scratch_shapes=[
            pltpu.VMEM((slots, nx + 2, nz + 2 * PAD, ny), f32),
            pltpu.VMEM((6, nx, nz, ny), f32),
            *[pltpu.VMEM((nx, nz, ny), f32) for _ in range(5)],
            pltpu.VMEM((slots, groups, TILE, LANES), f32),
            pltpu.VMEM((slots, 2, groups, TILE, LANES), f32),
            pltpu.VMEM((groups, TILE, LANES), f32),
            pltpu.VMEM((slots, 2, nx, ny), f32),
            pltpu.VMEM((slots, 2, nx, ny), f32),
            *[pltpu.VMEM((ITERS, count, DOT_ROWS, LANES), f32) for count in counts],
            pltpu.SemaphoreType.DMA((slots, 6)),
            pltpu.SemaphoreType.DMA((slots, 6)),
            pltpu.SemaphoreType.DMA((ITERS, links)),
            pltpu.SemaphoreType.DMA((ITERS, links)),
        ],
        compiler_params=pltpu.CompilerParams(
            collective_id=0, has_side_effects=True, vmem_limit_bytes=60 * 1024 * 1024),
    )(*turned)
    return tuple(jnp.swapaxes(value, 1, 2) for value in outs)


def solution(mesh):
    sizes = dict(mesh.shape)
    return jax.shard_map(
        functools.partial(local, sizes),
        mesh=mesh,
        in_specs=(P(*AXES), P(*AXES), P(*AXES)),
        out_specs=(P(*AXES), P(*AXES)),
        check_vma=False,
    )
```

```python
import functools
import math

import jax
import jax.numpy as jnp
from jax import lax
from jax.experimental import pallas as pl
from jax.experimental.pallas import tpu as pltpu
from jax.sharding import PartitionSpec as P

ITERS = 10
AXES = ("gx", "gy", "gz")
STAGES = (("gx", "gy", "gz"),)
MESH = pl.DeviceIdType.MESH
PAD = 8
TILE = 8
LANES = 128
HALF = LANES // 2
DOT_ROWS = 8


def kernel(sizes, b_ref, c_ref, a_ref, x_ref, r_ref,
           field, weight, diag, inverse, image_ref, direction_ref, along_ref,
           ysend, yrecv, yhalo, zsend, zrecv,
           parts_all, send_sem, recv_sem, sum_send, sum_recv):
    nx, nz, ny = x_ref.shape
    tiles = nz // TILE
    per_group = HALF // tiles
    groups = nx // per_group
    me = {axis: lax.axis_index(axis) for axis in AXES}
    inner = pl.ds(PAD, nz)

    barrier = pltpu.get_barrier_semaphore()
    def mine(axes):
        index, count = 0, 1
        for axis in axes:
            index = index * sizes[axis] + me[axis]
            count = count * sizes[axis]
        return index, count

    def place(axes, index):
        where = {}
        for axis in reversed(axes):
            where[axis] = lax.rem(index, sizes[axis])
            index = lax.div(index, sizes[axis])
        return where

    greeted = 0
    for axes in STAGES:
        index, count = mine(axes)
        for hop in range(1, count):
            peer = place(axes, lax.rem(index + hop, count))
            pl.semaphore_signal(barrier, inc=1, device_id=peer, device_id_type=MESH)
            greeted += 1
    pl.semaphore_wait(barrier, greeted)

    lane = lax.broadcasted_iota(jnp.int32, (TILE, LANES), 1)
    owner = ((lane + 1) // 2) % HALF
    even = lane % 2 == 0
    lane_wide = lax.broadcasted_iota(jnp.int32, (nz, LANES), 1)
    first, last = lane_wide == 0, lane_wide == LANES - 1

    def each_copy(slot, act):
        plan = {
            "gx": ((field.at[slot, 1, inner], field.at[slot, nx + 1, inner]),
                   (field.at[slot, nx, inner], field.at[slot, 0, inner])),
            "gy": ((ysend.at[slot], yrecv.at[slot, 1]), (ysend.at[slot], yrecv.at[slot, 0])),
            "gz": ((zsend.at[slot, 0], zrecv.at[slot, 1]), (zsend.at[slot, 1], zrecv.at[slot, 0])),
        }
        for number, axis in enumerate(AXES):
            for side in range(2):
                source, target = plan[axis][side]
                act(axis, side, source, target, slot, 2 * number + side)

    def descriptor(axis, side, source, target, slot, index):
        peer = me[axis] + (2 * side - 1)
        return pltpu.make_async_remote_copy(
            src_ref=source, dst_ref=target,
            send_sem=send_sem.at[slot, index], recv_sem=recv_sem.at[slot, index],
            device_id={axis: peer}, device_id_type=MESH)

    def has_peer(axis, side):
        return me[axis] > 0 if side == 0 else me[axis] < sizes[axis] - 1

    def start(axis, side, *rest):
        @pl.when(has_peer(axis, side))
        def _():
            descriptor(axis, side, *rest).start()

    def finish(axis, side, *rest):
        @pl.when(has_peer(axis, side))
        def _():
            descriptor(axis, side, *rest).wait_send()

        @pl.when(has_peer(axis, 1 - side))
        def _():
            descriptor(axis, side, *rest).wait_recv()

    def clear(slot, carry):
        plane = jnp.zeros((nz, ny), jnp.float32)
        for edge, at in ((me["gx"] == 0, 0), (me["gx"] == sizes["gx"] - 1, nx + 1)):
            @pl.when(edge)
            def _():
                field[slot, at, inner] = plane
        for edge, at in ((me["gy"] == 0, 0), (me["gy"] == sizes["gy"] - 1, 1)):
            @pl.when(edge)
            def _():
                yrecv[slot, at] = jnp.zeros(yrecv.shape[2:], jnp.float32)
        for edge, at in ((me["gz"] == 0, 0), (me["gz"] == sizes["gz"] - 1, 1)):
            @pl.when(edge)
            def _():
                zrecv[slot, at] = jnp.zeros(zrecv.shape[2:], jnp.float32)
        return carry

    lax.fori_loop(0, ITERS + 1, clear, 0)

    def put(slot, x, within, plane, packed):
        field[slot, x + 1, inner] = plane
        zsend[slot, 0, pl.ds(x, 1)] = plane[:1]
        zsend[slot, 1, pl.ds(x, 1)] = plane[nz - 1:]
        for tile in range(tiles):
            number = within * tiles + tile
            part = plane[tile * TILE:(tile + 1) * TILE]
            if number:
                part = pltpu.roll(part, 2 * number, 1)
            packed = jnp.where(owner == number, part, packed)
        return packed

    def exchange(slot):
        each_copy(slot, start)
        each_copy(slot, finish)
        for group in range(groups):
            yhalo[group] = jnp.where(even, pltpu.roll(yrecv[slot, 0, group], 1, 1),
                                     pltpu.roll(yrecv[slot, 1, group], LANES - 1, 1))
        for x in range(nx):
            field[slot, x + 1, PAD - 1:PAD] = zrecv[slot, 0, x:x + 1]
            field[slot, x + 1, PAD + nz:PAD + nz + 1] = zrecv[slot, 1, x:x + 1]

    def around(slot, x, group, within):
        here = field[slot, x + 1, inner]
        beside = yhalo[group]
        edge = []
        for tile in range(tiles):
            number = within * tiles + tile
            edge.append(pltpu.roll(beside, LANES - 2 * number, 1) if number else beside)
        edge = jnp.concatenate(edge, axis=0)
        return here, (
            field[slot, x + 2, inner],
            field[slot, x, inner],
            jnp.where(last, edge, pltpu.roll(here, LANES - 1, 1)),
            jnp.where(first, edge, pltpu.roll(here, 1, 1)),
            field[slot, x + 1, PAD + 1:PAD + 1 + nz],
            field[slot, x + 1, PAD - 1:PAD - 1 + nz],
        )

    def fold(plane):
        total = plane[:TILE]
        for tile in range(1, tiles):
            total = total + plane[tile * TILE:(tile + 1) * TILE]
        return total

    nothing = jnp.zeros((TILE, LANES), jnp.float32)

    def load(group, carry):
        packed = nothing
        for within in range(per_group):
            x = group * per_group + within
            packed = put(0, x, within, c_ref[x], packed)
        ysend[0, group] = packed
        return carry

    lax.fori_loop(0, groups, load, 0)
    exchange(0)

    def prepare(group, carry):
        packed = nothing
        for within in range(per_group):
            x = group * per_group + within
            here, neighbours = around(0, x, group, within)
            faces = [0.5 * (here + other) for other in neighbours]
            diagonal = a_ref[x]
            for number, face in enumerate(faces):
                diagonal = diagonal + face
                weight[number, x] = face
            diag[x] = diagonal
            reciprocal = 1.0 / diagonal
            inverse[x] = reciprocal
            source = b_ref[x]
            r_ref[x] = source
            blank = jnp.zeros_like(source)
            x_ref[x] = blank
            direction_ref[x] = blank
            along_ref[x] = blank
            packed = put(1, x, within, source * reciprocal, packed)
        ysend[1, group] = packed
        return carry

    lax.fori_loop(0, groups, prepare, 0)

    def all_sums(k, sums):
        base = 0
        for axes, parts in zip(STAGES, (parts_all,)):
            index, count = mine(axes)
            parts[k, index] = sums
            sends, arrivals = [], []
            for hop in range(1, count):
                behind = lax.rem(index + count - hop, count)
                ahead = lax.rem(index + hop, count)
                for whose, device, out in ((index, ahead, sends), (behind, behind, arrivals)):
                    out.append(pltpu.make_async_remote_copy(
                        src_ref=parts.at[k, whose], dst_ref=parts.at[k, whose],
                        send_sem=sum_send.at[k, base], recv_sem=sum_recv.at[k, base],
                        device_id=place(axes, device), device_id_type=MESH))
                base += 1
            for copy in sends:
                copy.start()
            for copy, arrival in zip(sends, arrivals):
                copy.wait_send()
                arrival.wait_recv()
            sums = parts[k, 0]
            for number in range(1, count):
                sums = sums + parts[k, number]
        return jnp.broadcast_to(jnp.sum(sums, axis=1, keepdims=True), (DOT_ROWS, LANES))

    def iteration(k, carry):
        rho_now, step_size = carry
        slot = k + 1
        exchange(slot)

        def apply(group, totals):
            rho_total, product_total = totals
            for within in range(per_group):
                x = group * per_group + within
                here, neighbours = around(slot, x, group, within)
                beside = weight[0, x] * neighbours[0]
                for number in range(1, 6):
                    beside = beside + weight[number, x] * neighbours[number]
                image = diag[x] * here - beside
                image_ref[x] = image
                rho_total = rho_total + fold(r_ref[x] * here)
                product_total = product_total + fold(image * here)
            return rho_total, product_total

        rho_total, product_total = lax.fori_loop(0, groups, apply, (nothing, nothing))
        sums = all_sums(k, jnp.concatenate([
            jnp.sum(rho_total, axis=0, keepdims=True),
            jnp.sum(product_total, axis=0, keepdims=True),
            jnp.zeros((DOT_ROWS - 2, LANES), jnp.float32)], axis=0))
        rho_next, product = sums[:1], sums[1:2]
        mixing = jnp.where(k == 0, 0.0, rho_next / rho_now)
        step_next = rho_next / (product - mixing * rho_next / step_size)

        def update(group, carry):
            packed = nothing
            for within in range(per_group):
                x = group * per_group + within
                direction = field[slot, x + 1, inner] + mixing * direction_ref[x]
                along = image_ref[x] + mixing * along_ref[x]
                direction_ref[x] = direction
                along_ref[x] = along
                x_ref[x] = x_ref[x] + step_next * direction
                residual = r_ref[x] - step_next * along
                r_ref[x] = residual
                packed = put(slot + 1, x, within, residual * inverse[x], packed)
            ysend[slot + 1, group] = packed
            return carry

        lax.fori_loop(0, groups, update, 0)
        return rho_next, step_next

    one = jnp.ones((1, LANES), jnp.float32)
    lax.fori_loop(0, ITERS, iteration, (one, one))


def local(sizes, right_side, conductivity, absorption):
    turned = [jnp.swapaxes(value, 1, 2) for value in (right_side, conductivity, absorption)]
    nx, nz, ny = turned[0].shape
    groups = nx * (nz // TILE) // HALF
    slots = ITERS + 2
    f32 = jnp.float32
    counts = [math.prod(sizes[axis] for axis in axes) for axes in STAGES]
    links = sum(count - 1 for count in counts)
    out = jax.ShapeDtypeStruct((nx, nz, ny), f32)
    vmem = pl.BlockSpec(memory_space=pltpu.VMEM)
    outs = pl.pallas_call(
        functools.partial(kernel, sizes),
        out_shape=(out, out),
        in_specs=[vmem] * 3,
        out_specs=(vmem, vmem),
        scratch_shapes=[
            pltpu.VMEM((slots, nx + 2, nz + 2 * PAD, ny), f32),
            pltpu.VMEM((6, nx, nz, ny), f32),
            *[pltpu.VMEM((nx, nz, ny), f32) for _ in range(5)],
            pltpu.VMEM((slots, groups, TILE, LANES), f32),
            pltpu.VMEM((slots, 2, groups, TILE, LANES), f32),
            pltpu.VMEM((groups, TILE, LANES), f32),
            pltpu.VMEM((slots, 2, nx, ny), f32),
            pltpu.VMEM((slots, 2, nx, ny), f32),
            *[pltpu.VMEM((ITERS, count, DOT_ROWS, LANES), f32) for count in counts],
            pltpu.SemaphoreType.DMA((slots, 6)),
            pltpu.SemaphoreType.DMA((slots, 6)),
            pltpu.SemaphoreType.DMA((ITERS, links)),
            pltpu.SemaphoreType.DMA((ITERS, links)),
        ],
        compiler_params=pltpu.CompilerParams(
            collective_id=0, has_side_effects=True, vmem_limit_bytes=60 * 1024 * 1024),
    )(*turned)
    return tuple(jnp.swapaxes(value, 1, 2) for value in outs)


def solution(mesh):
    sizes = dict(mesh.shape)
    return jax.shard_map(
        functools.partial(local, sizes),
        mesh=mesh,
        in_specs=(P(*AXES), P(*AXES), P(*AXES)),
        out_specs=(P(*AXES), P(*AXES)),
        check_vma=False,
    )
```
